256 devices in a mesh: depth: 16 (over z, core), tx: 4 (over y), ty: 4 (over x).
Axes of the slice: x: 4, y: 4, z: 8, core: 2. Of those that a mesh axis runs over, the one named last changes fastest.
Arguments:
- field: float32 [256, 256, 512], P('depth', 'tx', 'ty'), may hold values from -6 to 6
- shear: int32 [6, 256, 2], P(None, 'depth'), may hold values from 0 to 7
- fraction: float32 [6, 256, 2], P(None, 'depth'), may hold values from 0.05 to 0.95
- absorb: float32 [6], replicated, may hold values from 0.004 to 0.012
- palette: float32 [3, 3], replicated, may hold values from -1 to 1
- order: int32 [6], replicated, may hold values from 0 to 1, as said below
Outputs:
- image: float32 [6, 4, 256, 512], P(None, None, 'tx', 'ty')
The draws below stay inside these ranges and needn't reach their ends.
Inputs may be any that keep to these rules, and one draw needn't show every extreme that they name: `order`: both values occur among the 6 views.
All inputs are finite; a program needn't handle non-finite values.
Results may differ from the reference program's by a relative error of at most 0.0003.
Values sent between devices are 32-bit elements; how exact they have to be, the bound alone decides.
No kernel may reach another device: no remote copies, remote signals or barrier semaphores. Data moves between devices by JAX's collectives and lax.ppermute only.
A program may use at most 64 MiB of HBM per device.

```python
import math
import jax
import jax.numpy as jnp
from jax import lax

VIEWS = 6
SPILL = 8
NZ = 256
NX = 256
NY = 512


def draw_order(key, part):
    bit_key = jax.random.fold_in(key, 11)
    pick_key = jax.random.fold_in(key, 23)
    flags = jax.random.randint(bit_key, (VIEWS,), 0, 2).astype(jnp.int32)
    total = jnp.sum(flags)
    uniform_set = jnp.logical_or(total == 0, total == VIEWS)
    chosen = jax.random.randint(pick_key, (), 0, VIEWS).astype(jnp.int32)
    marked = jnp.arange(VIEWS, dtype=jnp.int32) == chosen
    flipped_flags = jnp.where(marked, 1 - flags, flags)
    return jnp.where(uniform_set, flipped_flags, flags).astype(jnp.int32)


def plant(drawn, own_key, least, top_value):
    spot = [jax.random.randint(jax.random.fold_in(own_key, axis), (), 0, length) for axis, length in enumerate(drawn.shape)]
    main_axis = drawn.shape.index(max(drawn.shape))
    next_to = spot[:main_axis] + [(spot[main_axis] + 1) % drawn.shape[main_axis]] + spot[main_axis + 1:]
    return drawn.at[tuple(spot)].set(least).at[tuple(next_to)].set(top_value)


def shard_levels(own_key, extent, shards, smallest, largest):
    gain, own = 1.0, jax.random.fold_in(own_key, 6)
    for position, blocks in shards:
        steps = jnp.exp(jax.random.uniform(jax.random.fold_in(own, position), (blocks,), jnp.float32, smallest / len(shards), largest / len(shards)))
        gain = gain * jnp.repeat(steps, extent[position] // blocks).reshape([-1 if axis == position else 1 for axis in range(len(extent))])
    return gain


def centred(stream_key, extent, deviation, reach, cuts=(), held_as=jnp.bfloat16):
    loudness = shard_levels(stream_key, extent, cuts, -0.22, 0.18) if cuts else 1.0
    values = jax.random.normal(stream_key, extent, jnp.float32) * deviation * loudness
    return jnp.minimum(jnp.maximum(values, -reach), reach).astype(held_as)


def setup_inputs(seed: int = 0) -> dict:
    key_list = jax.random.split(jax.random.key(seed), 7)
    return {
        "field": centred(key_list[0], (NZ, NX, NY), 1.0, 6.0, ((0, 16), (1, 4), (2, 4)), jnp.float32),
        "shear": plant(jax.random.randint(key_list[1], (VIEWS, NZ, 2), 0, SPILL), jax.random.fold_in(key_list[1], 1), 0, SPILL - 1).astype(jnp.int32),
        "fraction": jnp.clip(0.05 + 0.9 * jax.random.uniform(key_list[2], (VIEWS, NZ, 2), jnp.float32) ** shard_levels(key_list[2], (VIEWS, NZ, 2), ((1, 16),), -0.2, 0.2), 0.05, 0.95),
        "absorb": jnp.clip(jnp.exp(jax.random.uniform(key_list[3], (VIEWS,), jnp.float32, math.log(0.004), math.log(0.012))), 0.004, 0.012),
        "palette": jnp.clip(jax.random.uniform(key_list[4], (3, 3), jnp.float32, -1.0, 1.0), -1.0, 1.0),
        "order": draw_order(jax.random.fold_in(key_list[6], 71), 0),
    }


def shear_axis(values, offset, weight, axis_num):
    length = values.shape[axis_num]
    widths = [(0, 0)] * values.ndim
    widths[axis_num] = (SPILL, 0)
    padded = jnp.pad(values, widths)
    start = (SPILL - offset).astype(jnp.int32)
    nearer = lax.dynamic_slice_in_dim(padded, start, length, axis_num)
    farther = lax.dynamic_slice_in_dim(padded, (start - 1).astype(jnp.int32), length, axis_num)
    return (1.0 - weight) * nearer + weight * farther


def render_view(field, shear_row, fraction_row, absorb_val, palette, flipped):
    def advance(carried, step_idx):
        colour_sum, through = carried
        plane = jnp.where(flipped == 1, NZ - 1 - step_idx, step_idx).astype(jnp.int32)
        layer = lax.dynamic_index_in_dim(field, plane, 0, keepdims=False)
        offsets = lax.dynamic_index_in_dim(shear_row, plane, 0, keepdims=False)
        weights = lax.dynamic_index_in_dim(fraction_row, plane, 0, keepdims=False)
        sheared = shear_axis(layer, offsets[0], weights[0], 0)
        sheared = shear_axis(sheared, offsets[1], weights[1], 1)
        squared = sheared * sheared
        opacity = absorb_val * squared / (1.0 + squared)
        colour = palette[:, 0, None, None] + palette[:, 1, None, None] * sheared[None] + palette[:, 2, None, None] * squared[None]
        colour_sum = colour_sum + (through * opacity)[None] * colour
        through = through * (1.0 - opacity)
        return (colour_sum, through), None

    start_state = (jnp.zeros((3, NX, NY), jnp.float32), jnp.ones((NX, NY), jnp.float32))
    final_state, unused = lax.scan(advance, start_state, jnp.arange(NZ, dtype=jnp.int32))
    colour_sum, through = final_state
    return jnp.concatenate([colour_sum, (1.0 - through)[None]], 0)


def reference(field, shear, fraction, absorb, palette, order):
    images = []
    for view_idx in range(VIEWS):
        images.append(render_view(field, shear[view_idx], fraction[view_idx], absorb[view_idx], palette, order[view_idx]))
    return jnp.stack(images, 0)
```

```python
import jax
import jax.numpy as jnp
from jax import lax
from jax.experimental import pallas as pl
from jax.experimental.pallas import tpu as pltpu
from jax.sharding import PartitionSpec as P

VIEWS = 6
HALF = VIEWS // 2
SPILL = 8
LANES = 128


def vmem():
    return pl.BlockSpec(memory_space=pltpu.VMEM)


def smem():
    return pl.BlockSpec(memory_space=pltpu.SMEM)


def pack_kernel(field_ref, packed_ref):
    depth, rows, lanes = field_ref.shape
    lane = lax.broadcasted_iota(jnp.int32, (rows, lanes), 1)
    packed = jnp.zeros((rows, lanes), jnp.float32)
    for g in range(depth):
        moved = pltpu.roll(field_ref[g], (g * SPILL + SPILL) % lanes, 1)
        packed = jnp.where((lane >= g * SPILL) & (lane < (g + 1) * SPILL), moved, packed)
    packed_ref[...] = packed


def render_kernel(
    shear_ref, fraction_ref, absorb_ref, order_ref, field_ref, rows_ref, cols_ref, corner_ref,
    give_ref, keep_ref, shifted_ref,
):
    depth, rows, lanes = field_ref.shape
    core = lax.rem(lax.axis_index("depth"), 2)
    has_rows = lax.axis_index("tx") > 0
    has_cols = lax.axis_index("ty") > 0
    lane = lax.broadcasted_iota(jnp.int32, (rows + SPILL, lanes), 1)
    beside = jnp.concatenate(
        [jnp.where(has_rows, corner_ref[...], 0.0), cols_ref[...]], 0
    )
    beside = jnp.where(has_cols, beside, 0.0)

    def spread(g, carry):
        own = jnp.concatenate([jnp.where(has_rows, rows_ref[g], 0.0), field_ref[g]], 0)
        edge = pltpu.roll(beside, lanes - SPILL - g * SPILL, 1)
        shifted_ref[g, 0] = own
        for s in range(1, SPILL + 1):
            shifted_ref[g, s] = pltpu.roll(jnp.where(lane >= lanes - s, edge, own), s, 1)
        return carry

    lax.fori_loop(0, depth, spread, 0)

    def view(v, out_ref, k):
        absorb = absorb_ref[v]
        flipped = order_ref[v] == 1

        def one(i, carry):
            through, first, second = carry
            g = jnp.where(flipped, depth - 1 - i, i)
            o_row, o_col = shear_ref[v, g, 0], shear_ref[v, g, 1]
            f_row, f_col = fraction_ref[v, g, 0], fraction_ref[v, g, 1]
            near, far = SPILL - o_row, SPILL - 1 - o_row
            a = shifted_ref[g, o_col, pl.ds(near, rows), :]
            b = shifted_ref[g, o_col + 1, pl.ds(near, rows), :]
            c = shifted_ref[g, o_col, pl.ds(far, rows), :]
            d = shifted_ref[g, o_col + 1, pl.ds(far, rows), :]
            upper = (1.0 - f_col) * a + f_col * b
            lower = (1.0 - f_col) * c + f_col * d
            tile = (1.0 - f_row) * upper + f_row * lower
            squared = tile * tile
            opacity = absorb * squared / (1.0 + squared)
            weight = through * opacity
            return through - weight, first + weight * tile, second + weight * squared

        zero = jnp.zeros((rows, lanes), jnp.float32)
        through, first, second = lax.fori_loop(0, depth, one, (zero + 1.0, zero, zero))
        out_ref[k, 0] = through
        out_ref[k, 1] = first
        out_ref[k, 2] = second

    def give(k, carry):
        view((1 - core) * HALF + k, give_ref, k)
        return carry

    def keep(k, carry):
        view(core * HALF + k, keep_ref, k)
        return carry

    lax.fori_loop(0, HALF, give, 0)
    lax.fori_loop(0, HALF, keep, 0)


def over(mine, other, mine_first):
    first = mine_first[:, None, None]
    t_mine, t_other = mine[:, 0], other[:, 0]
    w_mine = jnp.where(first, 1.0, t_other)
    w_other = jnp.where(first, t_mine, 1.0)
    return jnp.stack(
        [
            t_mine * t_other,
            w_mine * mine[:, 1] + w_other * other[:, 1],
            w_mine * mine[:, 2] + w_other * other[:, 2],
        ],
        1,
    )


def along_z(partner):
    return [(2 * z + c, 2 * partner(z) + c) for z in range(8) for c in range(2)]


def split(value, upper):
    half = value.shape[2] // 2
    kept = lax.dynamic_slice_in_dim(value, upper * half, half, 2)
    sent = lax.dynamic_slice_in_dim(value, (1 - upper) * half, half, 2)
    return kept, sent


def join(mine, other, upper):
    return jnp.where(
        upper == 1, jnp.concatenate([other, mine], 2), jnp.concatenate([mine, other], 2)
    )


def shards(field, shear, fraction, absorb, palette, order):
    depth, rows, lanes = field.shape
    place = lax.axis_index("depth")
    core, z = place % 2, place // 2
    rank = jnp.where(z < 4, z, 7 - z)
    ring = [(i, (i + 1) % 4) for i in range(4)]
    diagonal = [(4 * i + j, (i + 1) % 4 * 4 + (j + 1) % 4) for i in range(4) for j in range(4)]

    packed = pl.pallas_call(
        pack_kernel,
        out_shape=jax.ShapeDtypeStruct((rows, lanes), jnp.float32),
        in_specs=[vmem()],
        out_specs=vmem(),
    )(field)
    row_halo = lax.ppermute(field[:, rows - SPILL:, :], "tx", ring)
    col_halo = lax.ppermute(packed, "ty", ring)
    corner = lax.ppermute(packed[rows - SPILL:], ("tx", "ty"), diagonal)

    part = jax.ShapeDtypeStruct((HALF, 3, rows, lanes), jnp.float32)
    give, keep = pl.pallas_call(
        render_kernel,
        out_shape=(part, part),
        in_specs=[smem()] * 4 + [vmem()] * 4,
        out_specs=(vmem(), vmem()),
        scratch_shapes=[pltpu.VMEM((depth, SPILL + 1, rows + SPILL, lanes), jnp.float32)],
    )(shear, fraction, absorb, order, field, row_halo, col_halo, corner)

    forward = lax.dynamic_slice_in_dim(order, core * HALF, HALF) == 0
    cores = [(i, i ^ 1) for i in range(16)]
    value = over(keep, lax.ppermute(give, "depth", cores), forward == (core == 0))

    near, second = along_z(lambda z: z ^ 1), along_z(lambda z: z ^ 2)
    mirror = along_z(lambda z: 7 - z)
    kept, sent = split(value, rank % 2)
    value = over(kept, lax.ppermute(sent, "depth", near), forward == (z % 2 == 0))
    kept, sent = split(value, rank // 2)
    value = over(kept, lax.ppermute(sent, "depth", second), forward == (z % 4 < 2))
    value = over(value, lax.ppermute(value, "depth", mirror), forward == (z < 4))
    value = join(value, lax.ppermute(value, "depth", second), rank // 2)
    value = join(value, lax.ppermute(value, "depth", near), rank % 2)
    other = lax.ppermute(value, "depth", cores)
    value = jnp.where(core == 1, jnp.concatenate([other, value], 0), jnp.concatenate([value, other], 0))

    alpha = 1.0 - value[:, 0]
    image = [
        palette[c, 0] * alpha + palette[c, 1] * value[:, 1] + palette[c, 2] * value[:, 2]
        for c in range(3)
    ]
    return jnp.stack(image + [alpha], 1)


def solution(mesh):
    return jax.shard_map(
        shards,
        mesh=mesh,
        in_specs=(
            P("depth", "tx", "ty"),
            P(None, "depth", None),
            P(None, "depth", None),
            P(),
            P(),
            P(),
        ),
        out_specs=P(None, None, "tx", "ty"),
        check_vma=False,
    )
```

```python
import jax
import jax.numpy as jnp
from jax import lax
from jax.experimental import pallas as pl
from jax.experimental.pallas import tpu as pltpu
from jax.sharding import PartitionSpec as P

VIEWS = 6
HALF = VIEWS // 2
SPILL = 8
LANES = 128


def vmem():
    return pl.BlockSpec(memory_space=pltpu.VMEM)


def smem():
    return pl.BlockSpec(memory_space=pltpu.SMEM)


def pack_kernel(field_ref, rows_ref, packed_ref, corner_ref):
    depth, rows, lanes = field_ref.shape
    rows_ref[...] = field_ref[:, rows - SPILL:, :]
    lane = lax.broadcasted_iota(jnp.int32, (rows, lanes), 1)
    packed = jnp.zeros((rows, lanes), jnp.float32)
    for g in range(depth):
        moved = pltpu.roll(field_ref[g], (g * SPILL + SPILL) % lanes, 1)
        packed = jnp.where(lane >= g * SPILL, moved, packed)
    packed_ref[...] = packed
    corner_ref[...] = packed[rows - SPILL:]


def render_kernel(
    shear_ref, fraction_ref, absorb_ref, order_ref, field_ref, rows_ref, cols_ref, corner_ref,
    give_ref, keep_ref, whole_ref, step_ref, beside_ref, beside_step_ref, even_ref, odd_ref,
):
    depth, rows, lanes = field_ref.shape
    tall = rows + SPILL
    core = lax.rem(lax.axis_index("depth"), 2)
    has_rows = lax.axis_index("tx") > 0
    has_cols = lax.axis_index("ty") > 0
    lane = lax.broadcasted_iota(jnp.int32, (tall, lanes), 1)
    beside = jnp.concatenate([jnp.where(has_rows, corner_ref[...], 0.0), cols_ref[...]], 0)
    beside = jnp.where(has_cols, beside, 0.0)
    beside_ref[...] = beside
    beside_step_ref[...] = pltpu.roll(beside, 1, 1) - beside

    def prepare(g, carry):
        own = jnp.concatenate([jnp.where(has_rows, rows_ref[g], 0.0), field_ref[g]], 0)
        edge = pltpu.roll(beside, lanes - SPILL - g * SPILL + 1, 1)
        before = jnp.where(lane == 0, edge, pltpu.roll(own, 1, 1))
        whole_ref[g] = own
        step_ref[g] = before - own
        return carry

    lax.fori_loop(0, depth, prepare, 0)
    group = lax.broadcasted_iota(jnp.int32, (SPILL, lanes), 1) // SPILL

    def edge_of(v):
        weight = jnp.zeros((SPILL, lanes), jnp.float32)
        for g in range(depth):
            weight = jnp.where(group == g, fraction_ref[v, 1, g], weight)
        weight = jnp.concatenate([weight] * (tall // SPILL), 0)
        return beside_ref[...] + weight * beside_step_ref[...]

    def columns(v, g, edge_ref, out_ref):
        offset = shear_ref[v, 1, g]
        mixed = whole_ref[g] + fraction_ref[v, 1, g] * step_ref[g]
        mixed = pltpu.roll(mixed, offset, 1)
        edge = pltpu.roll(edge_ref[...], lanes - SPILL - g * SPILL + offset, 1)
        out_ref[g] = jnp.where(lane < offset, edge, mixed)

    def shade(v, flipped, i, carry, in_ref):
        through, first, second = carry
        g = jnp.where(flipped, depth - 1 - i, i)
        offset, weight = shear_ref[v, 0, g], fraction_ref[v, 0, g]
        near = in_ref[g, pl.ds(SPILL - offset, rows), :]
        far = in_ref[g, pl.ds(SPILL - 1 - offset, rows), :]
        tile = near + weight * (far - near)
        squared = tile * tile
        opacity = absorb_ref[v] * squared / (1.0 + squared)
        lost = through * opacity
        return through - lost, first + lost * tile, second + lost * squared

    def view_of(k):
        return (1 - core) * HALF + k if k < HALF else core * HALF + k - HALF

    def scoped(edge_ref):
        def first_view(g, carry):
            columns(view_of(0), g, edge_ref, even_ref)
            return carry

        edge_ref[...] = edge_of(view_of(0))
        lax.fori_loop(0, depth, first_view, 0)
        zero = jnp.zeros((rows, lanes), jnp.float32)
        for k in range(VIEWS):
            v = view_of(k)
            flipped = order_ref[v] == 1
            here, there = (even_ref, odd_ref) if k % 2 == 0 else (odd_ref, even_ref)
            if k + 1 < VIEWS:
                edge_ref[...] = edge_of(view_of(k + 1))

            def one(i, carry):
                carry = shade(v, flipped, i, carry, here)
                if k + 1 < VIEWS:
                    columns(view_of(k + 1), i, edge_ref, there)
                return carry

            through, first, second = lax.fori_loop(0, depth, one, (zero + 1.0, zero, zero))
            out_ref = give_ref if k < HALF else keep_ref
            out_ref[k % HALF, 0] = through
            out_ref[k % HALF, 1] = first
            out_ref[k % HALF, 2] = second

    pl.run_scoped(scoped, pltpu.VMEM((tall, lanes), jnp.float32))


def paint_kernel(palette_ref, mine_ref, other_ref, image_ref):
    core = lax.rem(lax.axis_index("depth"), 2)
    for part_ref, base in ((mine_ref, core * HALF), (other_ref, (1 - core) * HALF)):
        for k in range(HALF):
            alpha = 1.0 - part_ref[k, 0]
            first, second = part_ref[k, 1], part_ref[k, 2]
            for c in range(3):
                image_ref[base + k, c] = (
                    palette_ref[c, 0] * alpha + palette_ref[c, 1] * first + palette_ref[c, 2] * second
                )
            image_ref[base + k, 3] = alpha


def over(mine, other, mine_first):
    first = mine_first[:, None, None]
    t_mine, t_other = mine[:, 0], other[:, 0]
    w_mine = jnp.where(first, 1.0, t_other)
    w_other = jnp.where(first, t_mine, 1.0)
    return jnp.stack(
        [
            t_mine * t_other,
            w_mine * mine[:, 1] + w_other * other[:, 1],
            w_mine * mine[:, 2] + w_other * other[:, 2],
        ],
        1,
    )


def along_z(partner):
    return [(2 * z + c, 2 * partner(z) + c) for z in range(8) for c in range(2)]


def split(value, upper):
    half = value.shape[2] // 2
    kept = lax.dynamic_slice_in_dim(value, upper * half, half, 2)
    sent = lax.dynamic_slice_in_dim(value, (1 - upper) * half, half, 2)
    return kept, sent


def join(mine, other, upper):
    return jnp.where(
        upper == 1, jnp.concatenate([other, mine], 2), jnp.concatenate([mine, other], 2)
    )


def shards(field, shear, fraction, absorb, palette, order):
    depth, rows, lanes = field.shape
    place = lax.axis_index("depth")
    core, z = place % 2, place // 2
    rank = jnp.where(z < 4, z, (z % 4) ^ 2)
    ring = [(i, (i + 1) % 4) for i in range(4)]
    diagonal = [(4 * i + j, (i + 1) % 4 * 4 + (j + 1) % 4) for i in range(4) for j in range(4)]

    small = pltpu.CompilerParams(vmem_limit_bytes=4 << 20)
    row_halo, packed, corner = pl.pallas_call(
        pack_kernel,
        out_shape=(
            jax.ShapeDtypeStruct((depth, SPILL, lanes), jnp.float32),
            jax.ShapeDtypeStruct((rows, lanes), jnp.float32),
            jax.ShapeDtypeStruct((SPILL, lanes), jnp.float32),
        ),
        in_specs=[vmem()],
        out_specs=(vmem(), vmem(), vmem()),
        compiler_params=small,
    )(field)
    row_halo = lax.ppermute(row_halo, "tx", ring)
    col_halo = lax.ppermute(packed, "ty", ring)
    corner = lax.ppermute(corner, ("tx", "ty"), diagonal)

    part = jax.ShapeDtypeStruct((HALF, 3, rows, lanes), jnp.float32)
    slab = pltpu.VMEM((depth, rows + SPILL, lanes), jnp.float32)
    strip = pltpu.VMEM((rows + SPILL, lanes), jnp.float32)
    give, keep = pl.pallas_call(
        render_kernel,
        out_shape=(part, part),
        in_specs=[smem()] * 4 + [vmem()] * 4,
        out_specs=(vmem(), vmem()),
        scratch_shapes=[slab, slab, strip, strip, slab, slab],
        compiler_params=pltpu.CompilerParams(vmem_limit_bytes=8 << 20),
    )(
        jnp.transpose(shear, (0, 2, 1)), jnp.transpose(fraction, (0, 2, 1)), absorb, order,
        field, row_halo, col_halo, corner,
    )

    forward = lax.dynamic_slice_in_dim(order, core * HALF, HALF) == 0
    cores = [(i, i ^ 1) for i in range(16)]
    value = over(keep, lax.ppermute(give, "depth", cores), forward == (core == 0))

    near, second = along_z(lambda z: z ^ 1), along_z(lambda z: z ^ 2)
    third = along_z(lambda z: z ^ 6)
    kept, sent = split(value, rank % 2)
    value = over(kept, lax.ppermute(sent, "depth", near), forward == (z % 2 == 0))
    kept, sent = split(value, rank // 2)
    value = over(kept, lax.ppermute(sent, "depth", second), forward == (z % 4 < 2))
    value = over(value, lax.ppermute(value, "depth", third), forward == (z < 4))
    value = join(value, lax.ppermute(value, "depth", second), rank // 2)
    value = join(value, lax.ppermute(value, "depth", near), rank % 2)
    other = lax.ppermute(value, "depth", cores)
    return pl.pallas_call(
        paint_kernel,
        out_shape=jax.ShapeDtypeStruct((VIEWS, 4, rows, lanes), jnp.float32),
        in_specs=[smem(), vmem(), vmem()],
        out_specs=vmem(),
        compiler_params=small,
    )(palette, value, other)


def solution(mesh):
    return jax.shard_map(
        shards,
        mesh=mesh,
        in_specs=(
            P("depth", "tx", "ty"),
            P(None, "depth", None),
            P(None, "depth", None),
            P(),
            P(),
            P(),
        ),
        out_specs=P(None, None, "tx", "ty"),
        check_vma=False,
    )
```

```python
import jax
import jax.numpy as jnp
from jax import lax
from jax.experimental import pallas as pl
from jax.experimental.pallas import tpu as pltpu
from jax.sharding import PartitionSpec as P

VIEWS = 6
HALF = VIEWS // 2
SPILL = 8
LANES = 128


def vmem():
    return pl.BlockSpec(memory_space=pltpu.VMEM)


def smem():
    return pl.BlockSpec(memory_space=pltpu.SMEM)


def pack_kernel(field_ref, rows_ref, packed_ref, corner_ref):
    depth, rows, lanes = field_ref.shape
    rows_ref[...] = field_ref[:, rows - SPILL:, :]
    lane = lax.broadcasted_iota(jnp.int32, (rows, lanes), 1)
    packed = jnp.zeros((rows, lanes), jnp.float32)
    for g in range(depth):
        moved = pltpu.roll(field_ref[g], (g * SPILL + SPILL) % lanes, 1)
        packed = jnp.where(lane >= g * SPILL, moved, packed)
    packed_ref[...] = packed
    corner_ref[...] = packed[rows - SPILL:]


def prepare(field_ref, rows_ref, cols_ref, corner_ref, table_ref):
    depth, rows, lanes = field_ref.shape
    has_rows = lax.axis_index("tx") > 0
    has_cols = lax.axis_index("ty") > 0
    last_lane = lax.broadcasted_iota(jnp.int32, (rows + SPILL, lanes), 1) == lanes - 1
    beside = jnp.concatenate([jnp.where(has_rows, corner_ref[...], 0.0), cols_ref[...]], 0)
    beside = jnp.where(has_cols, beside, 0.0)
    beside_step = pltpu.roll(beside, 1, 1) - beside

    for g in range(depth):
        own = jnp.concatenate([jnp.where(has_rows, rows_ref[g], 0.0), field_ref[g]], 0)
        turn = lanes - SPILL - g * SPILL
        edge = pltpu.roll(beside, turn, 1)
        before = pltpu.roll(jnp.where(last_lane, edge, own), 1, 1)
        table_ref[0, g] = own
        table_ref[1, g] = before - own
        table_ref[2, g] = edge
        table_ref[3, g] = pltpu.roll(beside_step, turn, 1)


def render(shear_ref, fraction_ref, absorb_ref, order_ref, table_ref, out_ref, base, mixed_refs):
    _, depth, tall, lanes = table_ref.shape
    rows = tall - SPILL
    lane = lax.broadcasted_iota(jnp.int32, (tall, lanes), 1)

    def view(k, carry):
        v = base + k
        flipped = order_ref[v] == 1
        absorb = absorb_ref[v]
        through = jnp.ones((rows, lanes), jnp.float32)
        first = second = jnp.zeros((rows, lanes), jnp.float32)

        def columns(i):
            g = jnp.where(flipped, depth - 1 - i, i)
            offset, weight = shear_ref[v, 1, g], fraction_ref[v, 1, g]
            outside = lane >= lanes - offset
            own = jnp.where(outside, table_ref[2, g], table_ref[0, g])
            step = jnp.where(outside, table_ref[3, g], table_ref[1, g])
            mixed_refs[i % len(mixed_refs)][...] = pltpu.roll(own + weight * step, offset, 1)

        def tile_of(i):
            g = jnp.where(flipped, depth - 1 - i, i)
            offset, weight = shear_ref[v, 0, g], fraction_ref[v, 0, g]
            mixed_ref = mixed_refs[i % len(mixed_refs)]
            near = mixed_ref[pl.ds(SPILL - offset, rows), :]
            far = mixed_ref[pl.ds(SPILL - 1 - offset, rows), :]
            return near + weight * (far - near)

        columns(0)
        for i in range(depth):
            if i + 1 < depth:
                columns(i + 1)
            tile = tile_of(i)
            squared = tile * tile
            lost = through * (absorb * squared / (1.0 + squared))
            through = through - lost
            first = first + lost * tile
            second = second + lost * squared
        out_ref[k, 0] = through
        out_ref[k, 1] = first
        out_ref[k, 2] = second
        return carry

    lax.fori_loop(0, HALF, view, 0)


def give_kernel(
    shear_ref, fraction_ref, absorb_ref, order_ref, field_ref, rows_ref, cols_ref, corner_ref,
    out_ref, table_ref, *mixed_refs,
):
    prepare(field_ref, rows_ref, cols_ref, corner_ref, table_ref)
    base = (1 - lax.rem(lax.axis_index("depth"), 2)) * HALF
    render(shear_ref, fraction_ref, absorb_ref, order_ref, table_ref, out_ref, base, mixed_refs)


def keep_kernel(shear_ref, fraction_ref, absorb_ref, order_ref, table_ref, out_ref, *mixed_refs):
    base = lax.rem(lax.axis_index("depth"), 2) * HALF
    render(shear_ref, fraction_ref, absorb_ref, order_ref, table_ref, out_ref, base, mixed_refs)


def paint_kernel(palette_ref, mine_ref, other_ref, image_ref):
    core = lax.rem(lax.axis_index("depth"), 2)
    for part_ref, base in ((mine_ref, core * HALF), (other_ref, (1 - core) * HALF)):
        for k in range(HALF):
            alpha = 1.0 - part_ref[k, 0]
            first, second = part_ref[k, 1], part_ref[k, 2]
            for c in range(3):
                image_ref[base + k, c] = (
                    palette_ref[c, 0] * alpha + palette_ref[c, 1] * first + palette_ref[c, 2] * second
                )
            image_ref[base + k, 3] = alpha


def over(mine, other, mine_first):
    first = mine_first[:, None, None]
    t_mine, t_other = mine[:, 0], other[:, 0]
    w_mine = jnp.where(first, 1.0, t_other)
    w_other = jnp.where(first, t_mine, 1.0)
    return jnp.stack(
        [
            t_mine * t_other,
            w_mine * mine[:, 1] + w_other * other[:, 1],
            w_mine * mine[:, 2] + w_other * other[:, 2],
        ],
        1,
    )


def along_z(partner):
    return [(2 * z + c, 2 * partner(z) + c) for z in range(8) for c in range(2)]


def split(value, upper):
    half = value.shape[2] // 2
    kept = lax.dynamic_slice_in_dim(value, upper * half, half, 2)
    sent = lax.dynamic_slice_in_dim(value, (1 - upper) * half, half, 2)
    return kept, sent


def join(mine, other, upper):
    return jnp.where(
        upper == 1, jnp.concatenate([other, mine], 2), jnp.concatenate([mine, other], 2)
    )


def shards(field, shear, fraction, absorb, palette, order):
    depth, rows, lanes = field.shape
    place = lax.axis_index("depth")
    core, z = place % 2, place // 2
    rank = jnp.where(z < 4, z, (z % 4) ^ 2)
    ring = [(i, (i + 1) % 4) for i in range(4)]
    diagonal = [(4 * i + j, (i + 1) % 4 * 4 + (j + 1) % 4) for i in range(4) for j in range(4)]

    small = pltpu.CompilerParams(vmem_limit_bytes=4 << 20)
    row_halo, packed, corner = pl.pallas_call(
        pack_kernel,
        out_shape=(
            jax.ShapeDtypeStruct((depth, SPILL, lanes), jnp.float32),
            jax.ShapeDtypeStruct((rows, lanes), jnp.float32),
            jax.ShapeDtypeStruct((SPILL, lanes), jnp.float32),
        ),
        in_specs=[vmem()],
        out_specs=(vmem(), vmem(), vmem()),
        compiler_params=small,
    )(field)
    row_halo = lax.ppermute(row_halo, "tx", ring)
    col_halo = lax.ppermute(packed, "ty", ring)
    corner = lax.ppermute(corner, ("tx", "ty"), diagonal)

    part = jax.ShapeDtypeStruct((HALF, 3, rows, lanes), jnp.float32)
    tables = (jnp.transpose(shear, (0, 2, 1)), jnp.transpose(fraction, (0, 2, 1)), absorb, order)
    scratch = [pltpu.VMEM((rows + SPILL, lanes), jnp.float32)] * 4
    give, table = pl.pallas_call(
        give_kernel,
        out_shape=(part, jax.ShapeDtypeStruct((4, depth, rows + SPILL, lanes), jnp.float32)),
        in_specs=[smem()] * 4 + [vmem()] * 4,
        out_specs=(vmem(), vmem()),
        scratch_shapes=scratch,
        compiler_params=small,
    )(*tables, field, row_halo, col_halo, corner)
    keep = pl.pallas_call(
        keep_kernel,
        out_shape=part,
        in_specs=[smem()] * 4 + [vmem()],
        out_specs=vmem(),
        scratch_shapes=scratch,
        compiler_params=small,
    )(*tables, table)

    forward = lax.dynamic_slice_in_dim(order, core * HALF, HALF) == 0
    cores = [(i, i ^ 1) for i in range(16)]
    value = over(keep, lax.ppermute(give, "depth", cores), forward == (core == 0))

    near, second = along_z(lambda z: z ^ 1), along_z(lambda z: z ^ 2)
    third = along_z(lambda z: z ^ 6)
    kept, sent = split(value, rank % 2)
    value = over(kept, lax.ppermute(sent, "depth", near), forward == (z % 2 == 0))
    kept, sent = split(value, rank // 2)
    value = over(kept, lax.ppermute(sent, "depth", second), forward == (z % 4 < 2))
    value = over(value, lax.ppermute(value, "depth", third), forward == (z < 4))
    value = join(value, lax.ppermute(value, "depth", second), rank // 2)
    value = join(value, lax.ppermute(value, "depth", near), rank % 2)
    other = lax.ppermute(value, "depth", cores)
    return pl.pallas_call(
        paint_kernel,
        out_shape=jax.ShapeDtypeStruct((VIEWS, 4, rows, lanes), jnp.float32),
        in_specs=[smem(), vmem(), vmem()],
        out_specs=vmem(),
        compiler_params=small,
    )(palette, value, other)


def solution(mesh):
    return jax.shard_map(
        shards,
        mesh=mesh,
        in_specs=(
            P("depth", "tx", "ty"),
            P(None, "depth", None),
            P(None, "depth", None),
            P(),
            P(),
            P(),
        ),
        out_specs=P(None, None, "tx", "ty"),
        check_vma=False,
    )
```

```python
import jax
import jax.numpy as jnp
from jax import lax
from jax.experimental import pallas as pl
from jax.experimental.pallas import tpu as pltpu
from jax.sharding import PartitionSpec as P

VIEWS = 6
HALF = VIEWS // 2
SPILL = 8
STREAMS = 1
LANES = 128


def vmem():
    return pl.BlockSpec(memory_space=pltpu.VMEM)


def smem():
    return pl.BlockSpec(memory_space=pltpu.SMEM)


def hbm():
    return pl.BlockSpec(memory_space=pltpu.HBM)


def pack_kernel(field_ref, rows_ref, packed_ref, corner_ref):
    depth, rows, lanes = field_ref.shape
    rows_ref[...] = field_ref[:, rows - SPILL:, :]
    lane = lax.broadcasted_iota(jnp.int32, (rows, lanes), 1)
    packed = jnp.zeros((rows, lanes), jnp.float32)
    for g in range(depth):
        moved = pltpu.roll(field_ref[g], (g * SPILL + SPILL) % lanes, 1)
        packed = jnp.where(lane >= g * SPILL, moved, packed)
    packed_ref[...] = packed
    corner_ref[...] = packed[rows - SPILL:]


def begin_kernel(field_ref, table_ref):
    rows = field_ref.shape[1]
    for g in range(field_ref.shape[0]):
        own = field_ref[g]
        table_ref[0, g, pl.ds(SPILL, rows), :] = own
        table_ref[1, g, pl.ds(SPILL, rows), :] = pltpu.roll(own, 1, 1) - own


def prepare(begun_ref, rows_ref, cols_ref, corner_ref, table_ref):
    _, depth, tall, lanes = table_ref.shape
    rows = tall - SPILL
    has_rows = lax.axis_index("tx") > 0
    has_cols = lax.axis_index("ty") > 0
    first_lane = lax.broadcasted_iota(jnp.int32, (tall, lanes), 1) == 0
    beside = jnp.concatenate([jnp.where(has_rows, corner_ref[...], 0.0), cols_ref[...]], 0)
    beside = jnp.where(has_cols, beside, 0.0)
    shifted = pltpu.roll(beside, 1, 1)

    for g in range(depth):
        turn = lanes - SPILL - g * SPILL
        edge = pltpu.roll(beside, turn, 1)
        before = pltpu.roll(shifted, turn, 1)
        above = jnp.where(has_rows, rows_ref[g], 0.0)
        own = begun_ref[0, g, pl.ds(SPILL, rows), :]
        step = jnp.concatenate([pltpu.roll(above, 1, 1) - above, begun_ref[1, g, pl.ds(SPILL, rows), :]], 0)
        own = jnp.concatenate([above, own], 0)
        table_ref[0, g] = own
        table_ref[1, g] = jnp.where(first_lane, before - own, step)
        table_ref[2, g] = edge
        table_ref[3, g] = before - edge


def render(whole_ref, parts_ref, table_ref, out_ref, base, mixed_refs):
    _, depth, tall, lanes = table_ref.shape
    rows = tall - SPILL
    lane = lax.broadcasted_iota(jnp.int32, (tall, lanes), 1)

    def view(k, carry):
        v = base + k
        flipped = whole_ref[v, 0, depth] == 1
        absorb = parts_ref[v, 0, depth]
        through = jnp.ones((rows, lanes), jnp.float32)
        first = second = jnp.zeros((rows, lanes), jnp.float32)

        def columns(i):
            g = jnp.where(flipped, depth - 1 - i, i)
            offset, weight = whole_ref[v, 1, g], parts_ref[v, 1, g]
            outside = lane >= lanes - offset
            own = jnp.where(outside, table_ref[2, g], table_ref[0, g])
            step = jnp.where(outside, table_ref[3, g], table_ref[1, g])
            mixed_refs[i % len(mixed_refs)][...] = pltpu.roll(own + weight * step, offset, 1)

        def tile_of(i):
            g = jnp.where(flipped, depth - 1 - i, i)
            offset, weight = whole_ref[v, 0, g], parts_ref[v, 0, g]
            mixed_ref = mixed_refs[i % len(mixed_refs)]
            near = mixed_ref[pl.ds(SPILL - offset, rows), :]
            far = mixed_ref[pl.ds(SPILL - 1 - offset, rows), :]
            return near + weight * (far - near)

        columns(0)
        for i in range(depth):
            if i + 1 < depth:
                columns(i + 1)
            tile = tile_of(i)
            squared = tile * tile
            lost = through * (absorb * squared / (1.0 + squared))
            through = through - lost
            first = first + lost * tile
            second = second + lost * squared
        out_ref[k, 0] = through
        out_ref[k, 1] = first
        out_ref[k, 2] = second
        return carry

    lax.fori_loop(0, HALF, view, 0)


def give_kernel(whole_ref, parts_ref, begun_ref, rows_ref, cols_ref, corner_ref, out_ref, table_ref, *mixed_refs):
    prepare(begun_ref, rows_ref, cols_ref, corner_ref, table_ref)
    base = (1 - lax.rem(lax.axis_index("depth"), 2)) * HALF
    render(whole_ref, parts_ref, table_ref, out_ref, base, mixed_refs)


def keep_kernel(whole_ref, parts_ref, table_ref, out_ref, *mixed_refs):
    base = lax.rem(lax.axis_index("depth"), 2) * HALF
    render(whole_ref, parts_ref, table_ref, out_ref, base, mixed_refs)


def paint_kernel(palette_ref, *refs):
    parts, (image_ref, canvas_ref, sems) = refs[:-3], refs[-3:]
    height = parts[0].shape[2]
    core = lax.rem(lax.axis_index("depth"), 2)
    copies = []
    for side in range(2):
        base = (core if side == 0 else 1 - core) * HALF
        for k in range(HALF):
            n = len(copies)
            for stream in range(STREAMS):
                part_ref = parts[side * STREAMS + stream]
                band = pl.ds(stream * height, height)
                alpha = 1.0 - part_ref[k, 0]
                first, second = part_ref[k, 1], part_ref[k, 2]
                for c in range(3):
                    canvas_ref[n, c, band, :] = (
                        palette_ref[c, 0] * alpha + palette_ref[c, 1] * first + palette_ref[c, 2] * second
                    )
                canvas_ref[n, 3, band, :] = alpha
            copies.append(pltpu.make_async_copy(canvas_ref.at[n], image_ref.at[base + k], sems.at[n]))
            copies[-1].start()
    for copy in copies:
        copy.wait()


def over(mine, other, mine_first):
    first = mine_first[:, None, None]
    t_mine, t_other = mine[:, 0], other[:, 0]
    w_mine = jnp.where(first, 1.0, t_other)
    w_other = jnp.where(first, t_mine, 1.0)
    return jnp.stack(
        [
            t_mine * t_other,
            w_mine * mine[:, 1] + w_other * other[:, 1],
            w_mine * mine[:, 2] + w_other * other[:, 2],
        ],
        1,
    )


def along_z(partner):
    return [(2 * z + c, 2 * partner(z) + c) for z in range(8) for c in range(2)]


def join(mine, other, upper):
    return jnp.where(
        upper == 1, jnp.concatenate([other, mine], 2), jnp.concatenate([mine, other], 2)
    )


def shards(field, shear, fraction, absorb, palette, order):
    depth, rows, lanes = field.shape
    place = lax.axis_index("depth")
    core, z = place % 2, place // 2
    rank = jnp.where(z < 4, z, (z % 4) ^ 2)
    ring = [(i, (i + 1) % 4) for i in range(4)]
    diagonal = [(4 * i + j, (i + 1) % 4 * 4 + (j + 1) % 4) for i in range(4) for j in range(4)]

    small = pltpu.CompilerParams(vmem_limit_bytes=4 << 20)
    row_halo, packed, corner = pl.pallas_call(
        pack_kernel,
        out_shape=(
            jax.ShapeDtypeStruct((depth, SPILL, lanes), jnp.float32),
            jax.ShapeDtypeStruct((rows, lanes), jnp.float32),
            jax.ShapeDtypeStruct((SPILL, lanes), jnp.float32),
        ),
        in_specs=[vmem()],
        out_specs=(vmem(), vmem(), vmem()),
        compiler_params=small,
    )(field)
    row_halo = lax.ppermute(row_halo, "tx", ring)
    col_halo = lax.ppermute(packed, "ty", ring)
    corner = lax.ppermute(corner, ("tx", "ty"), diagonal)

    def array(*shape):
        return jax.ShapeDtypeStruct(shape, jnp.float32)

    begun = pl.pallas_call(
        begin_kernel,
        out_shape=array(4, depth, rows + SPILL, lanes),
        in_specs=[vmem()],
        out_specs=vmem(),
        compiler_params=small,
        cost_estimate=pl.CostEstimate(flops=1000000, bytes_accessed=2000000, transcendentals=0),
    )(field)

    last = lax.broadcasted_iota(jnp.int32, (VIEWS, 2, depth + 1), 2) == depth

    def with_last(values, extra):
        values = jnp.pad(jnp.transpose(values, (0, 2, 1)), ((0, 0), (0, 0), (0, 1)))
        return jnp.where(last, extra[:, None, None], values)

    tables = (with_last(shear, order), with_last(fraction, absorb))
    part = array(HALF, 3, rows, lanes)
    scratch = [pltpu.VMEM((rows + SPILL, lanes), jnp.float32)] * 4
    give, table = pl.pallas_call(
        give_kernel,
        out_shape=(part, array(4, depth, rows + SPILL, lanes)),
        in_specs=[smem()] * 2 + [vmem()] * 4,
        out_specs=(vmem(),) * 2,
        scratch_shapes=scratch,
        input_output_aliases={2: 1},
        compiler_params=small,
    )(*tables, begun, row_halo, col_halo, corner)
    keep = pl.pallas_call(
        keep_kernel,
        out_shape=part,
        in_specs=[smem()] * 2 + [vmem()],
        out_specs=vmem(),
        scratch_shapes=scratch,
        compiler_params=small,
        cost_estimate=pl.CostEstimate(flops=10000000, bytes_accessed=5000000, transcendentals=0),
    )(*tables, table)

    forward = lax.dynamic_slice_in_dim(tables[0][:, 0, depth], core * HALF, HALF) == 0
    cores = [(i, i ^ 1) for i in range(16)]
    full = over(keep, lax.ppermute(give, "depth", cores), forward == (core == 0))

    height = rows // 4
    within = [along_z(lambda z, step=step: z ^ step) for step in range(4)]
    across = along_z(lambda z: z ^ 6)

    def quarter(step):
        return lax.dynamic_slice_in_dim(full, (rank ^ step) * height, height, 2)

    came = [quarter(0)] + [None] * 3
    for step in (3, 2, 1):
        came[step] = lax.ppermute(quarter(step), "depth", within[step])
    even = forward == (z % 2 == 0)
    value = over(over(came[0], came[1], even), over(came[2], came[3], even), forward == (z % 4 < 2))
    value = over(value, lax.ppermute(value, "depth", across), forward == (z < 4))
    came = [value] + [None] * 3
    for step in (3, 2, 1):
        came[step] = lax.ppermute(value, "depth", within[step])
    value = join(join(came[0], came[1], rank % 2), join(came[2], came[3], rank % 2), rank // 2)
    values, others = [value], [lax.ppermute(value, "depth", cores)]
    return pl.pallas_call(
        paint_kernel,
        out_shape=array(VIEWS, 4, rows, lanes),
        in_specs=[smem()] + [vmem()] * (2 * STREAMS),
        out_specs=hbm(),
        scratch_shapes=[
            pltpu.VMEM((VIEWS, 4, rows, lanes), jnp.float32),
            pltpu.SemaphoreType.DMA((VIEWS,)),
        ],
        compiler_params=pltpu.CompilerParams(vmem_limit_bytes=6 << 20),
    )(palette, *values, *others)


def solution(mesh):
    return jax.shard_map(
        shards,
        mesh=mesh,
        in_specs=(
            P("depth", "tx", "ty"),
            P(None, "depth", None),
            P(None, "depth", None),
            P(),
            P(),
            P(),
        ),
        out_specs=P(None, None, "tx", "ty"),
        check_vma=False,
    )
```

```python
import jax
import jax.numpy as jnp
from jax import lax
from jax.experimental import pallas as pl
from jax.experimental.pallas import tpu as pltpu
from jax.sharding import PartitionSpec as P

VIEWS = 6
HALF = VIEWS // 2
SPILL = 8


def vmem():
    return pl.BlockSpec(memory_space=pltpu.VMEM)


def smem():
    return pl.BlockSpec(memory_space=pltpu.SMEM)


def hbm():
    return pl.BlockSpec(memory_space=pltpu.HBM)


def pack_kernel(field_ref, held_ref, rows_ref, packed_ref, corner_ref):
    depth, rows, lanes = field_ref.shape
    held_ref[...] = field_ref[...]
    rows_ref[...] = field_ref[:, rows - SPILL:, :]
    lane = lax.broadcasted_iota(jnp.int32, (rows, lanes), 1)
    packed = jnp.zeros((rows, lanes), jnp.float32)
    for g in range(depth):
        moved = pltpu.roll(field_ref[g], (g * SPILL + SPILL) % lanes, 1)
        packed = jnp.where(lane >= g * SPILL, moved, packed)
    packed_ref[...] = packed
    corner_ref[...] = packed[rows - SPILL:]


def begin_kernel(field_ref, table_ref):
    rows = field_ref.shape[1]
    for g in range(field_ref.shape[0]):
        own = field_ref[g]
        table_ref[0, g, pl.ds(SPILL, rows), :] = own
        table_ref[1, g, pl.ds(SPILL, rows), :] = pltpu.roll(own, 1, 1) - own


def prepare(begun_ref, rows_ref, cols_ref, corner_ref, table_ref):
    _, depth, tall, lanes = table_ref.shape
    rows = tall - SPILL
    has_rows = lax.axis_index("tx") > 0
    has_cols = lax.axis_index("ty") > 0
    first_lane = lax.broadcasted_iota(jnp.int32, (tall, lanes), 1) == 0
    beside = jnp.concatenate([jnp.where(has_rows, corner_ref[...], 0.0), cols_ref[...]], 0)
    beside = jnp.where(has_cols, beside, 0.0)
    shifted = pltpu.roll(beside, 1, 1)

    for g in range(depth):
        turn = lanes - SPILL - g * SPILL
        edge = pltpu.roll(beside, turn, 1)
        before = pltpu.roll(shifted, turn, 1)
        above = jnp.where(has_rows, rows_ref[g], 0.0)
        own = begun_ref[0, g, pl.ds(SPILL, rows), :]
        step = jnp.concatenate([pltpu.roll(above, 1, 1) - above, begun_ref[1, g, pl.ds(SPILL, rows), :]], 0)
        own = jnp.concatenate([above, own], 0)
        table_ref[0, g] = own
        table_ref[1, g] = jnp.where(first_lane, before - own, step)
        table_ref[2, g] = edge
        table_ref[3, g] = before - edge


def spot():
    place = lax.axis_index("depth")
    core, z = lax.rem(place, 2), lax.div(place, 2)
    rank = jnp.where(z < 4, z, 7 - z)
    return core, z, lax.rem(rank, 2), lax.div(rank, 2)


def render(whole_ref, parts_ref, table_ref, out_ref, base, mixed_refs):
    _, depth, tall, lanes = table_ref.shape
    rows = tall - SPILL
    lane = lax.broadcasted_iota(jnp.int32, (tall, lanes), 1)

    def view(k, carry):
        v = base + k
        flipped = whole_ref[v, 0, depth] == 1
        absorb = parts_ref[v, 0, depth]
        through = jnp.ones((rows, lanes), jnp.float32)
        first = second = jnp.zeros((rows, lanes), jnp.float32)

        def columns(i):
            g = jnp.where(flipped, depth - 1 - i, i)
            offset, weight = whole_ref[v, 1, g], parts_ref[v, 1, g]
            outside = lane >= lanes - offset
            own = jnp.where(outside, table_ref[2, g], table_ref[0, g])
            step = jnp.where(outside, table_ref[3, g], table_ref[1, g])
            mixed_refs[i % len(mixed_refs)][...] = pltpu.roll(own + weight * step, offset, 1)

        def tile_of(i):
            g = jnp.where(flipped, depth - 1 - i, i)
            offset, weight = whole_ref[v, 0, g], parts_ref[v, 0, g]
            mixed_ref = mixed_refs[i % len(mixed_refs)]
            near = mixed_ref[pl.ds(SPILL - offset, rows), :]
            far = mixed_ref[pl.ds(SPILL - 1 - offset, rows), :]
            return near + weight * (far - near)

        columns(0)
        for i in range(depth):
            if i + 1 < depth:
                columns(i + 1)
            tile = tile_of(i)
            squared = tile * tile
            lost = through * (absorb * squared / (1.0 + squared))
            through = through - lost
            first = first + lost * tile
            second = second + lost * squared
        out_ref[k, 0] = through
        out_ref[k, 1] = first
        out_ref[k, 2] = second
        return carry

    lax.fori_loop(0, HALF, view, 0)


def give_kernel(whole_ref, parts_ref, begun_ref, rows_ref, cols_ref, corner_ref, out_ref, table_ref, *mixed_refs):
    prepare(begun_ref, rows_ref, cols_ref, corner_ref, table_ref)
    render(whole_ref, parts_ref, table_ref, out_ref, (1 - spot()[0]) * HALF, mixed_refs)


def keep_kernel(whole_ref, parts_ref, table_ref, out_ref, *mixed_refs):
    render(whole_ref, parts_ref, table_ref, out_ref, spot()[0] * HALF, mixed_refs)


def paint_kernel(palette_ref, mine_ref, other_ref, image_ref, canvas_ref, sems):
    core = spot()[0]
    copies = []
    for part_ref, base in ((mine_ref, core * HALF), (other_ref, (1 - core) * HALF)):
        for k in range(HALF):
            n = len(copies)
            alpha = 1.0 - part_ref[k, 0]
            first, second = part_ref[k, 1], part_ref[k, 2]
            for c in range(3):
                canvas_ref[n, c] = (
                    palette_ref[c, 0] * alpha + palette_ref[c, 1] * first + palette_ref[c, 2] * second
                )
            canvas_ref[n, 3] = alpha
            copies.append(pltpu.make_async_copy(canvas_ref.at[n], image_ref.at[base + k], sems.at[n]))
            copies[-1].start()
    for copy in copies:
        copy.wait()


def over(mine, other, mine_first):
    first = mine_first[:, None, None]
    t_mine, t_other = mine[:, 0], other[:, 0]
    w_mine = jnp.where(first, 1.0, t_other)
    w_other = jnp.where(first, t_mine, 1.0)
    return jnp.stack(
        [
            t_mine * t_other,
            w_mine * mine[:, 1] + w_other * other[:, 1],
            w_mine * mine[:, 2] + w_other * other[:, 2],
        ],
        1,
    )


def along_z(partner):
    return [(2 * z + c, 2 * partner(z) + c) for z in range(8) for c in range(2)]


def join(mine, other, upper):
    return jnp.where(
        upper == 1, jnp.concatenate([other, mine], 2), jnp.concatenate([mine, other], 2)
    )


def shards(field, shear, fraction, absorb, palette, order):
    depth, rows, lanes = field.shape
    ring = [(i, (i + 1) % 4) for i in range(4)]
    diagonal = [(4 * i + j, 4 * i + j + 5) for i in range(3) for j in range(3)]
    diagonal += [(12, 4), (7, 3), (15, 12), (3, 0), (13, 1), (14, 2), (11, 8)]

    small = pltpu.CompilerParams(vmem_limit_bytes=4 << 20)
    held, row_halo, packed, corner = pl.pallas_call(
        pack_kernel,
        out_shape=(
            jax.ShapeDtypeStruct((depth, rows, lanes), jnp.float32),
            jax.ShapeDtypeStruct((depth, SPILL, lanes), jnp.float32),
            jax.ShapeDtypeStruct((rows, lanes), jnp.float32),
            jax.ShapeDtypeStruct((SPILL, lanes), jnp.float32),
        ),
        in_specs=[vmem()],
        out_specs=(vmem(),) * 4,
        compiler_params=small,
    )(field)
    row_halo = lax.ppermute(row_halo, "tx", ring)
    col_halo = lax.ppermute(packed, "ty", ring)
    corner = lax.ppermute(corner, ("tx", "ty"), diagonal)

    def array(*shape):
        return jax.ShapeDtypeStruct(shape, jnp.float32)

    begun = pl.pallas_call(
        begin_kernel,
        out_shape=array(4, depth, rows + SPILL, lanes),
        in_specs=[vmem()],
        out_specs=vmem(),
        compiler_params=small,
        cost_estimate=pl.CostEstimate(flops=1000000, bytes_accessed=2000000, transcendentals=0),
    )(held)

    last = lax.broadcasted_iota(jnp.int32, (VIEWS, 2, depth + 1), 2) == depth

    def with_last(values, extra):
        values = jnp.pad(jnp.transpose(values, (0, 2, 1)), ((0, 0), (0, 0), (0, 1)))
        return jnp.where(last, extra[:, None, None], values)

    tables = (with_last(shear, order), with_last(fraction, absorb))
    part = array(HALF, 3, rows, lanes)
    scratch = [pltpu.VMEM((rows + SPILL, lanes), jnp.float32)] * 4
    give, table = pl.pallas_call(
        give_kernel,
        out_shape=(part, array(4, depth, rows + SPILL, lanes)),
        in_specs=[smem()] * 2 + [vmem()] * 4,
        out_specs=(vmem(),) * 2,
        scratch_shapes=scratch,
        input_output_aliases={2: 1},
        compiler_params=small,
    )(*tables, begun, row_halo, col_halo, corner)
    keep = pl.pallas_call(
        keep_kernel,
        out_shape=part,
        in_specs=[smem()] * 2 + [vmem()],
        out_specs=vmem(),
        scratch_shapes=scratch,
        compiler_params=small,
        cost_estimate=pl.CostEstimate(flops=10000000, bytes_accessed=5000000, transcendentals=0),
    )(*tables, table)

    core, z, odd, half = spot()
    forward = lax.dynamic_slice_in_dim(tables[0][:, 0, depth], core * HALF, HALF) == 0
    cores = [(i, i ^ 1) for i in range(16)]
    full = over(keep, lax.ppermute(give, "depth", cores), forward == (core == 0))

    height = rows // 4
    within = [along_z(lambda z, step=step: z ^ step) for step in range(4)]

    def quarter(step):
        return lax.dynamic_slice_in_dim(full, ((2 * half + odd) ^ step) * height, height, 2)

    came = [quarter(0)]
    for step in (1, 2, 3):
        came.append(lax.ppermute(quarter(step), "depth", within[step]))
    even = forward == (z % 2 == 0)
    value = over(over(came[0], came[1], even), over(came[2], came[3], even), forward == (z % 4 < 2))
    value = over(value, lax.ppermute(value, "depth", along_z(lambda z: 7 - z)), forward == (z < 4))
    came = [value]
    for step in (1, 2, 3):
        came.append(lax.ppermute(value, "depth", within[step]))
    mine = join(join(came[0], came[1], odd), join(came[2], came[3], odd), half)
    return pl.pallas_call(
        paint_kernel,
        out_shape=array(VIEWS, 4, rows, lanes),
        in_specs=[smem(), vmem(), vmem()],
        out_specs=hbm(),
        scratch_shapes=[pltpu.VMEM((VIEWS, 4, rows, lanes), jnp.float32), pltpu.SemaphoreType.DMA((VIEWS,))],
        compiler_params=pltpu.CompilerParams(vmem_limit_bytes=6 << 20),
    )(palette, mine, lax.ppermute(mine, "depth", cores))


def solution(mesh):
    return jax.shard_map(
        shards,
        mesh=mesh,
        in_specs=(
            P("depth", "tx", "ty"),
            P(None, "depth", None),
            P(None, "depth", None),
            P(),
            P(),
            P(),
        ),
        out_specs=P(None, None, "tx", "ty"),
        check_vma=False,
    )
```

```python
import jax
import jax.numpy as jnp
from jax import lax
from jax.experimental import pallas as pl
from jax.experimental.pallas import tpu as pltpu
from jax.sharding import PartitionSpec as P

VIEWS = 6
HALF = VIEWS // 2
SPILL = 8


def vmem():
    return pl.BlockSpec(memory_space=pltpu.VMEM)


def smem():
    return pl.BlockSpec(memory_space=pltpu.SMEM)


def hbm():
    return pl.BlockSpec(memory_space=pltpu.HBM)


def pack_kernel(field_ref, held_ref, rows_ref, packed_ref, corner_ref):
    depth, rows, lanes = field_ref.shape
    held_ref[...] = field_ref[...]
    rows_ref[...] = field_ref[:, rows - SPILL:, :]
    lane = lax.broadcasted_iota(jnp.int32, (rows, lanes), 1)
    packed = jnp.zeros((rows, lanes), jnp.float32)
    for g in range(depth):
        moved = pltpu.roll(field_ref[g], (g * SPILL + SPILL) % lanes, 1)
        packed = jnp.where(lane >= g * SPILL, moved, packed)
    packed_ref[...] = packed
    corner_ref[...] = packed[rows - SPILL:]


def begin_kernel(field_ref, table_ref, first_ref):
    depth, rows, lanes = field_ref.shape
    lane = lax.broadcasted_iota(jnp.int32, (rows, lanes), 1)
    first = jnp.zeros((rows, lanes), jnp.float32)
    for g in range(depth):
        own = field_ref[g]
        table_ref[0, g, pl.ds(SPILL, rows), :] = own
        table_ref[1, g, pl.ds(SPILL, rows), :] = pltpu.roll(own, 1, 1) - own
        first = jnp.where(lane >= g * SPILL, pltpu.roll(own, g * SPILL + SPILL - 1, 1), first)
    first_ref[...] = first


def prepare(rows_ref, cols_ref, corner_ref, first_ref, table_ref, edge_ref):
    _, depth, tall, lanes = table_ref.shape
    has_rows = lax.axis_index("tx") > 0
    has_cols = lax.axis_index("ty") > 0
    beside = jnp.concatenate([jnp.where(has_rows, corner_ref[...], 0.0), cols_ref[...]], 0)
    beside = jnp.where(has_cols, beside, 0.0)
    lane = lax.broadcasted_iota(jnp.int32, (SPILL, lanes), 1)
    first = jnp.zeros((SPILL, lanes), jnp.float32)
    for g in range(depth):
        above = jnp.where(has_rows, rows_ref[g], 0.0)
        table_ref[0, g, pl.ds(0, SPILL), :] = above
        table_ref[1, g, pl.ds(0, SPILL), :] = pltpu.roll(above, 1, 1) - above
        first = jnp.where(lane >= g * SPILL, pltpu.roll(above, g * SPILL + SPILL - 1, 1), first)
    first = jnp.concatenate([first, first_ref[...]], 0)
    lane = lax.broadcasted_iota(jnp.int32, (tall, lanes), 1)
    edge = jnp.where(lane % SPILL == SPILL - 1, first, pltpu.roll(beside, lanes - 1, 1))
    edge_ref[0] = edge
    edge_ref[1] = beside - edge


def spot():
    place = lax.axis_index("depth")
    core, z = lax.rem(place, 2), lax.div(place, 2)
    rank = jnp.where(z < 4, z, 7 - z)
    return core, z, lax.rem(rank, 2), lax.div(rank, 2)


def render(whole_ref, parts_ref, table_ref, edge_ref, out_ref, base, strip_ref, mixed_refs):
    _, depth, tall, lanes = table_ref.shape
    rows = tall - SPILL
    lane = lax.broadcasted_iota(jnp.int32, (tall, lanes), 1)
    group = lax.broadcasted_iota(jnp.int32, (SPILL, lanes), 1) // SPILL

    def view(k, carry):
        v = base + k
        flipped = whole_ref[v, 0, depth] == 1
        absorb = parts_ref[v, 0, depth]
        through = jnp.ones((rows, lanes), jnp.float32)
        first = second = jnp.zeros((rows, lanes), jnp.float32)
        weights = jnp.zeros((SPILL, lanes), jnp.float32)
        for g in range(depth):
            weights = jnp.where(group == g, parts_ref[v, 1, g], weights)
        weights = jnp.concatenate([weights] * (tall // SPILL), 0)
        strip_ref[...] = edge_ref[0] + weights * edge_ref[1]

        def columns(i):
            g = jnp.where(flipped, depth - 1 - i, i)
            offset, weight = whole_ref[v, 1, g], parts_ref[v, 1, g]
            mixed = pltpu.roll(table_ref[0, g] + weight * table_ref[1, g], offset, 1)
            strip = pltpu.roll(strip_ref[...], lax.rem(lanes + 1 - SPILL - g * SPILL + offset, lanes), 1)
            mixed_refs[i % len(mixed_refs)][...] = mixed
            pltpu.store(mixed_refs[i % len(mixed_refs)], strip, mask=lane <= offset)

        def tile_of(i):
            g = jnp.where(flipped, depth - 1 - i, i)
            offset, weight = whole_ref[v, 0, g], parts_ref[v, 0, g]
            mixed_ref = mixed_refs[i % len(mixed_refs)]
            near = mixed_ref[pl.ds(SPILL - offset, rows), :]
            far = mixed_ref[pl.ds(SPILL - 1 - offset, rows), :]
            return near + weight * (far - near)

        columns(0)
        for i in range(depth):
            if i + 1 < depth:
                columns(i + 1)
            tile = tile_of(i)
            squared = tile * tile
            lost = through * (absorb * squared / (1.0 + squared))
            through = through - lost
            first = first + lost * tile
            second = second + lost * squared
        out_ref[k, 0] = through
        out_ref[k, 1] = first
        out_ref[k, 2] = second
        return carry

    lax.fori_loop(0, HALF, view, 0)


def give_kernel(
    whole_ref, parts_ref, begun_ref, first_ref, rows_ref, cols_ref, corner_ref,
    out_ref, table_ref, edge_ref, strip_ref, *mixed_refs,
):
    prepare(rows_ref, cols_ref, corner_ref, first_ref, table_ref, edge_ref)
    base = (1 - spot()[0]) * HALF
    render(whole_ref, parts_ref, table_ref, edge_ref, out_ref, base, strip_ref, mixed_refs)


def keep_kernel(whole_ref, parts_ref, table_ref, edge_ref, out_ref, strip_ref, *mixed_refs):
    render(whole_ref, parts_ref, table_ref, edge_ref, out_ref, spot()[0] * HALF, strip_ref, mixed_refs)


def paint_kernel(palette_ref, mine_ref, other_ref, image_ref, canvas_ref, sems):
    core = spot()[0]
    copies = []
    for part_ref, base in ((mine_ref, core * HALF), (other_ref, (1 - core) * HALF)):
        for k in range(HALF):
            n = len(copies)
            alpha = 1.0 - part_ref[k, 0]
            first, second = part_ref[k, 1], part_ref[k, 2]
            for c in range(3):
                canvas_ref[n, c] = (
                    palette_ref[c, 0] * alpha + palette_ref[c, 1] * first + palette_ref[c, 2] * second
                )
            canvas_ref[n, 3] = alpha
            copies.append(pltpu.make_async_copy(canvas_ref.at[n], image_ref.at[base + k], sems.at[n]))
            copies[-1].start()
    for copy in copies:
        copy.wait()


def over(mine, other, mine_first):
    first = mine_first[:, None, None]
    t_mine, t_other = mine[:, 0], other[:, 0]
    w_mine = jnp.where(first, 1.0, t_other)
    w_other = jnp.where(first, t_mine, 1.0)
    return jnp.stack(
        [
            t_mine * t_other,
            w_mine * mine[:, 1] + w_other * other[:, 1],
            w_mine * mine[:, 2] + w_other * other[:, 2],
        ],
        1,
    )


def along_z(partner):
    return [(2 * z + c, 2 * partner(z) + c) for z in range(8) for c in range(2)]


def join(mine, other, upper):
    return jnp.where(
        upper == 1, jnp.concatenate([other, mine], 2), jnp.concatenate([mine, other], 2)
    )


def shards(field, shear, fraction, absorb, palette, order):
    depth, rows, lanes = field.shape
    ring = [(i, (i + 1) % 4) for i in range(4)]
    diagonal = [(4 * i + j, 4 * i + j + 5) for i in range(3) for j in range(3)]
    diagonal += [(12, 4), (7, 3), (15, 12), (3, 0), (13, 1), (14, 2), (11, 8)]

    small = pltpu.CompilerParams(vmem_limit_bytes=4 << 20)
    held, row_halo, packed, corner = pl.pallas_call(
        pack_kernel,
        out_shape=(
            jax.ShapeDtypeStruct((depth, rows, lanes), jnp.float32),
            jax.ShapeDtypeStruct((depth, SPILL, lanes), jnp.float32),
            jax.ShapeDtypeStruct((rows, lanes), jnp.float32),
            jax.ShapeDtypeStruct((SPILL, lanes), jnp.float32),
        ),
        in_specs=[vmem()],
        out_specs=(vmem(),) * 4,
        compiler_params=small,
    )(field)
    row_halo = lax.ppermute(row_halo, "tx", ring)
    col_halo = lax.ppermute(packed, "ty", ring)
    corner = lax.ppermute(corner, ("tx", "ty"), diagonal)

    def array(*shape):
        return jax.ShapeDtypeStruct(shape, jnp.float32)

    begun, first = pl.pallas_call(
        begin_kernel,
        out_shape=(array(2, depth, rows + SPILL, lanes), array(rows, lanes)),
        in_specs=[vmem()],
        out_specs=(vmem(),) * 2,
        compiler_params=small,
        cost_estimate=pl.CostEstimate(flops=1000000, bytes_accessed=2000000, transcendentals=0),
    )(held)

    last = lax.broadcasted_iota(jnp.int32, (VIEWS, 2, depth + 1), 2) == depth

    def with_last(values, extra):
        values = jnp.pad(jnp.transpose(values, (0, 2, 1)), ((0, 0), (0, 0), (0, 1)))
        return jnp.where(last, extra[:, None, None], values)

    tables = (with_last(shear, order), with_last(fraction, absorb))
    part = array(HALF, 3, rows, lanes)
    rendering = pltpu.CompilerParams(vmem_limit_bytes=4 << 20)
    scratch = [pltpu.VMEM((rows + SPILL, lanes), jnp.float32)] * 5
    give, table, edge = pl.pallas_call(
        give_kernel,
        out_shape=(part, array(2, depth, rows + SPILL, lanes), array(2, rows + SPILL, lanes)),
        in_specs=[smem()] * 2 + [vmem()] * 5,
        out_specs=(vmem(),) * 3,
        scratch_shapes=scratch,
        input_output_aliases={2: 1},
        compiler_params=rendering,
    )(*tables, begun, first, row_halo, col_halo, corner)
    keep = pl.pallas_call(
        keep_kernel,
        out_shape=part,
        in_specs=[smem()] * 2 + [vmem()] * 2,
        out_specs=vmem(),
        scratch_shapes=scratch,
        compiler_params=rendering,
        cost_estimate=pl.CostEstimate(flops=10000000, bytes_accessed=5000000, transcendentals=0),
    )(*tables, table, edge)

    core, z, odd, half = spot()
    forward = lax.dynamic_slice_in_dim(tables[0][:, 0, depth], core * HALF, HALF) == 0
    cores = [(i, i ^ 1) for i in range(16)]
    full = over(keep, lax.ppermute(give, "depth", cores), forward == (core == 0))

    height = rows // 4
    within = [along_z(lambda z, step=step: z ^ step) for step in range(4)]

    def quarter(step):
        return lax.dynamic_slice_in_dim(full, ((2 * half + odd) ^ step) * height, height, 2)

    came = [quarter(0)]
    for step in (1, 2, 3):
        came.append(lax.ppermute(quarter(step), "depth", within[step]))
    even = forward == (z % 2 == 0)
    value = over(over(came[0], came[1], even), over(came[2], came[3], even), forward == (z % 4 < 2))
    value = over(value, lax.ppermute(value, "depth", along_z(lambda z: 7 - z)), forward == (z < 4))
    came = [value]
    for step in (1, 2, 3):
        came.append(lax.ppermute(value, "depth", within[step]))
    mine = join(join(came[0], came[1], odd), join(came[2], came[3], odd), half)
    return pl.pallas_call(
        paint_kernel,
        out_shape=array(VIEWS, 4, rows, lanes),
        in_specs=[smem(), vmem(), vmem()],
        out_specs=hbm(),
        scratch_shapes=[pltpu.VMEM((VIEWS, 4, rows, lanes), jnp.float32), pltpu.SemaphoreType.DMA((VIEWS,))],
        compiler_params=pltpu.CompilerParams(vmem_limit_bytes=6 << 20),
    )(palette, mine, lax.ppermute(mine, "depth", cores))


def solution(mesh):
    return jax.shard_map(
        shards,
        mesh=mesh,
        in_specs=(
            P("depth", "tx", "ty"),
            P(None, "depth", None),
            P(None, "depth", None),
            P(),
            P(),
            P(),
        ),
        out_specs=P(None, None, "tx", "ty"),
        check_vma=False,
    )
```

```python
import jax
import jax.numpy as jnp
from jax import lax
from jax.experimental import pallas as pl
from jax.experimental.pallas import tpu as pltpu
from jax.sharding import PartitionSpec as P

VIEWS = 6
HALF = VIEWS // 2
SPILL = 8


def vmem():
    return pl.BlockSpec(memory_space=pltpu.VMEM)


def smem():
    return pl.BlockSpec(memory_space=pltpu.SMEM)


def hbm():
    return pl.BlockSpec(memory_space=pltpu.HBM)


def pack_kernel(field_ref, held_ref, rows_ref, packed_ref, corner_ref):
    depth, rows, lanes = field_ref.shape
    held_ref[...] = field_ref[...]
    rows_ref[...] = field_ref[:, rows - SPILL:, :]
    lane = lax.broadcasted_iota(jnp.int32, (rows, lanes), 1)
    packed = jnp.zeros((rows, lanes), jnp.float32)
    for g in range(depth):
        moved = pltpu.roll(field_ref[g], (g * SPILL + SPILL) % lanes, 1)
        packed = jnp.where(lane >= g * SPILL, moved, packed)
    packed_ref[...] = packed
    corner_ref[...] = packed[rows - SPILL:]


def begin_kernel(field_ref, table_ref, first_ref):
    depth, rows, lanes = field_ref.shape
    lane = lax.broadcasted_iota(jnp.int32, (rows, lanes), 1)
    first = jnp.zeros((rows, lanes), jnp.float32)
    for g in range(depth):
        own = field_ref[g]
        table_ref[0, g, pl.ds(SPILL, rows), :] = own
        table_ref[1, g, pl.ds(SPILL, rows), :] = pltpu.roll(own, 1, 1) - own
        first = jnp.where(lane >= g * SPILL, pltpu.roll(own, g * SPILL + SPILL - 1, 1), first)
    first_ref[...] = first


def prepare(rows_ref, cols_ref, corner_ref, first_ref, table_ref, edge_ref):
    _, depth, tall, lanes = table_ref.shape
    has_rows = lax.axis_index("tx") > 0
    has_cols = lax.axis_index("ty") > 0
    beside = jnp.concatenate([jnp.where(has_rows, corner_ref[...], 0.0), cols_ref[...]], 0)
    beside = jnp.where(has_cols, beside, 0.0)
    lane = lax.broadcasted_iota(jnp.int32, (SPILL, lanes), 1)
    first = jnp.zeros((SPILL, lanes), jnp.float32)
    for g in range(depth):
        above = jnp.where(has_rows, rows_ref[g], 0.0)
        table_ref[0, g, pl.ds(0, SPILL), :] = above
        table_ref[1, g, pl.ds(0, SPILL), :] = pltpu.roll(above, 1, 1) - above
        first = jnp.where(lane >= g * SPILL, pltpu.roll(above, g * SPILL + SPILL - 1, 1), first)
    first = jnp.concatenate([first, first_ref[...]], 0)
    lane = lax.broadcasted_iota(jnp.int32, (tall, lanes), 1)
    edge = jnp.where(lane % SPILL == SPILL - 1, first, pltpu.roll(beside, lanes - 1, 1))
    edge_ref[0] = edge
    edge_ref[1] = beside - edge


def spot():
    place = lax.axis_index("depth")
    core, z = lax.rem(place, 2), lax.div(place, 2)
    rank = jnp.where(z < 4, z, 7 - z)
    return core, z, lax.rem(rank, 2), lax.div(rank, 2)


def render(whole_ref, parts_ref, table_ref, edge_ref, out_ref, base, strip_ref, mixed_refs):
    _, depth, tall, lanes = table_ref.shape
    rows = tall - SPILL
    lane = lax.broadcasted_iota(jnp.int32, (tall, lanes), 1)
    group = lax.broadcasted_iota(jnp.int32, (SPILL, lanes), 1) // SPILL

    def view(k, carry):
        v = base + k
        flipped = whole_ref[v, 0, depth] == 1
        absorb = parts_ref[v, 0, depth]
        through = jnp.ones((rows, lanes), jnp.float32)
        first = second = jnp.zeros((rows, lanes), jnp.float32)
        weights = jnp.zeros((SPILL, lanes), jnp.float32)
        for g in range(depth):
            weights = jnp.where(group == g, parts_ref[v, 1, g], weights)
        weights = jnp.concatenate([weights] * (tall // SPILL), 0)
        strip_ref[...] = edge_ref[0] + weights * edge_ref[1]

        def columns(i):
            g = jnp.where(flipped, depth - 1 - i, i)
            offset, weight = whole_ref[v, 1, g], parts_ref[v, 1, g]
            mixed = pltpu.roll(table_ref[0, g] + weight * table_ref[1, g], offset, 1)
            strip = pltpu.roll(strip_ref[...], lax.rem(lanes + 1 - SPILL - g * SPILL + offset, lanes), 1)
            mixed_refs[i % len(mixed_refs)][...] = mixed
            pltpu.store(mixed_refs[i % len(mixed_refs)], strip, mask=lane <= offset)

        def tile_of(i):
            g = jnp.where(flipped, depth - 1 - i, i)
            offset, weight = whole_ref[v, 0, g], parts_ref[v, 0, g]
            mixed_ref = mixed_refs[i % len(mixed_refs)]
            near = mixed_ref[pl.ds(SPILL - offset, rows), :]
            far = mixed_ref[pl.ds(SPILL - 1 - offset, rows), :]
            return near + weight * (far - near)

        columns(0)
        for i in range(depth):
            if i + 1 < depth:
                columns(i + 1)
            tile = tile_of(i)
            squared = tile * tile
            lost = through * (absorb * squared / (1.0 + squared))
            through = through - lost
            first = first + lost * tile
            second = second + lost * squared
        out_ref[k, 0] = through
        out_ref[k, 1] = first
        out_ref[k, 2] = second
        return carry

    lax.fori_loop(0, HALF, view, 0)


def give_kernel(
    whole_ref, parts_ref, begun_ref, first_ref, rows_ref, cols_ref, corner_ref,
    out_ref, table_ref, edge_ref, forward_ref, strip_ref, *mixed_refs,
):
    prepare(rows_ref, cols_ref, corner_ref, first_ref, table_ref, edge_ref)
    core, depth = spot()[0], table_ref.shape[1]
    for k in range(HALF):
        forward = jnp.where(whole_ref[core * HALF + k, 0, depth] == 0, 1.0, 0.0)
        forward_ref[k] = jnp.full(forward_ref.shape[1:], forward, jnp.float32)
    base = (1 - core) * HALF
    render(whole_ref, parts_ref, table_ref, edge_ref, out_ref, base, strip_ref, mixed_refs)


def keep_kernel(whole_ref, parts_ref, table_ref, edge_ref, out_ref, strip_ref, *mixed_refs):
    render(whole_ref, parts_ref, table_ref, edge_ref, out_ref, spot()[0] * HALF, strip_ref, mixed_refs)


def paint_kernel(palette_ref, *refs):
    parts, (image_ref, canvas_ref, sems) = refs[:4], refs[4:]
    core, _, _, half = spot()
    height = parts[0].shape[2]
    copies = []
    for side, base in ((0, core * HALF), (2, (1 - core) * HALF)):
        for k in range(HALF):
            n = len(copies)
            for part_ref, top in ((parts[side], half), (parts[side + 1], 1 - half)):
                band = pl.ds(pl.multiple_of(top * height, SPILL), height)
                alpha = 1.0 - part_ref[k, 0]
                first, second = part_ref[k, 1], part_ref[k, 2]
                for c in range(3):
                    canvas_ref[n, c, band, :] = (
                        palette_ref[c, 0] * alpha + palette_ref[c, 1] * first + palette_ref[c, 2] * second
                    )
                canvas_ref[n, 3, band, :] = alpha
            copies.append(pltpu.make_async_copy(canvas_ref.at[n], image_ref.at[base + k], sems.at[n]))
            copies[-1].start()
    for copy in copies:
        copy.wait()


def over(mine, other, mine_first):
    t_mine, t_other = mine[:, 0], other[:, 0]
    w_mine = jnp.where(mine_first, 1.0, t_other)
    w_other = jnp.where(mine_first, t_mine, 1.0)
    return jnp.stack(
        [
            t_mine * t_other,
            w_mine * mine[:, 1] + w_other * other[:, 1],
            w_mine * mine[:, 2] + w_other * other[:, 2],
        ],
        1,
    )


def along_z(partner):
    return [(2 * z + c, 2 * partner(z) + c) for z in range(8) for c in range(2)]


def join(mine, other, upper):
    return jnp.where(
        upper == 1, jnp.concatenate([other, mine], 2), jnp.concatenate([mine, other], 2)
    )


def shards(field, shear, fraction, absorb, palette, order):
    depth, rows, lanes = field.shape
    ring = [(i, (i + 1) % 4) for i in range(4)]
    diagonal = [(4 * i + j, 4 * i + j + 5) for i in range(3) for j in range(3)]
    diagonal += [(12, 4), (7, 3), (15, 12), (3, 0), (13, 1), (14, 2), (11, 8)]

    small = pltpu.CompilerParams(vmem_limit_bytes=4 << 20)
    held, row_halo, packed, corner = pl.pallas_call(
        pack_kernel,
        out_shape=(
            jax.ShapeDtypeStruct((depth, rows, lanes), jnp.float32),
            jax.ShapeDtypeStruct((depth, SPILL, lanes), jnp.float32),
            jax.ShapeDtypeStruct((rows, lanes), jnp.float32),
            jax.ShapeDtypeStruct((SPILL, lanes), jnp.float32),
        ),
        in_specs=[vmem()],
        out_specs=(vmem(),) * 4,
        compiler_params=small,
    )(field)
    row_halo = lax.ppermute(row_halo, "tx", ring)
    col_halo = lax.ppermute(packed, "ty", ring)
    corner = lax.ppermute(corner, ("tx", "ty"), diagonal)

    def array(*shape):
        return jax.ShapeDtypeStruct(shape, jnp.float32)

    begun, first = pl.pallas_call(
        begin_kernel,
        out_shape=(array(2, depth, rows + SPILL, lanes), array(rows, lanes)),
        in_specs=[vmem()],
        out_specs=(vmem(),) * 2,
        compiler_params=small,
        cost_estimate=pl.CostEstimate(flops=1000000, bytes_accessed=2000000, transcendentals=0),
    )(held)

    last = lax.broadcasted_iota(jnp.int32, (VIEWS, 2, depth + 1), 2) == depth

    def with_last(values, extra):
        values = jnp.pad(jnp.transpose(values, (0, 2, 1)), ((0, 0), (0, 0), (0, 1)))
        return jnp.where(last, extra[:, None, None], values)

    tables = (with_last(shear, order), with_last(fraction, absorb))
    part = array(HALF, 3, rows, lanes)
    rendering = pltpu.CompilerParams(vmem_limit_bytes=4 << 20)
    scratch = [pltpu.VMEM((rows + SPILL, lanes), jnp.float32)] * 5
    give, table, edge, forward = pl.pallas_call(
        give_kernel,
        out_shape=(part, array(2, depth, rows + SPILL, lanes), array(2, rows + SPILL, lanes), array(HALF, SPILL, lanes)),
        in_specs=[smem()] * 2 + [vmem()] * 5,
        out_specs=(vmem(),) * 4,
        scratch_shapes=scratch,
        input_output_aliases={2: 1},
        compiler_params=rendering,
    )(*tables, begun, first, row_halo, col_halo, corner)
    keep = pl.pallas_call(
        keep_kernel,
        out_shape=part,
        in_specs=[smem()] * 2 + [vmem()] * 2,
        out_specs=vmem(),
        scratch_shapes=scratch,
        compiler_params=rendering,
        cost_estimate=pl.CostEstimate(flops=10000000, bytes_accessed=5000000, transcendentals=0),
    )(*tables, table, edge)

    core, z, odd, half = spot()
    cores = [(i, i ^ 1) for i in range(16)]

    def nearer(lower):
        return (forward[:, :1] > 0.5) == lower

    full = over(keep, lax.ppermute(give, "depth", cores), nearer(core == 0))

    height = rows // 4
    within = [along_z(lambda z, step=step: z ^ step) for step in range(4)]

    def quarter(step):
        return lax.dynamic_slice_in_dim(full, ((2 * half + odd) ^ step) * height, height, 2)

    came = [quarter(0)]
    for step in (1, 2, 3):
        came.append(lax.ppermute(quarter(step), "depth", within[step]))
    even = nearer(z % 2 == 0)
    value = over(over(came[0], came[1], even), over(came[2], came[3], even), nearer(z % 4 < 2))
    value = over(value, lax.ppermute(value, "depth", along_z(lambda z: 7 - z)), nearer(z < 4))
    came = [value]
    for step in (1, 2, 3):
        came.append(lax.ppermute(value, "depth", within[step]))
    mine = [join(came[n], came[n + 1], odd) for n in (0, 2)]
    other = [lax.ppermute(rows_, "depth", cores) for rows_ in mine]
    return pl.pallas_call(
        paint_kernel,
        out_shape=array(VIEWS, 4, rows, lanes),
        in_specs=[smem()] + [vmem()] * 4,
        out_specs=hbm(),
        scratch_shapes=[pltpu.VMEM((VIEWS, 4, rows, lanes), jnp.float32), pltpu.SemaphoreType.DMA((VIEWS,))],
        compiler_params=pltpu.CompilerParams(vmem_limit_bytes=6 << 20),
    )(palette, *mine, *other)


def solution(mesh):
    return jax.shard_map(
        shards,
        mesh=mesh,
        in_specs=(
            P("depth", "tx", "ty"),
            P(None, "depth", None),
            P(None, "depth", None),
            P(),
            P(),
            P(),
        ),
        out_specs=P(None, None, "tx", "ty"),
        check_vma=False,
    )
```
